32 devices in a mesh: dp: 8 (over y, x, core), ctx: 4 (over z).
Axes of the slice: x: 2, y: 2, z: 4, core: 2. Of those that a mesh axis runs over, the one named last changes fastest.
Arguments:
- tokens: bfloat16 [16, 2048, 1088], P('dp', 'ctx'), may hold values from -6 to 6
- segments: int32 [16, 2048], P('dp'), may hold values from 0 to 31, never falling along the last dimension, each value on 1 to 1024 neighbouring positions
- adapter_index: int32 [16], P('dp'), may hold values from 0 to 7
- w_qkv: bfloat16 [1088, 3264], P('ctx', 'dp'), may hold values from -0.1875 to 0.1875
- w_out: bfloat16 [1088, 1088], P('ctx', 'dp'), may hold values from -0.75 to 0.75
- w_fc1: bfloat16 [1088, 4352], P('ctx', 'dp'), may hold values from -0.1875 to 0.1875
- w_fc2: bfloat16 [4352, 1088], P('ctx', 'dp'), may hold values from -0.09375 to 0.09375
- gain_one: float32 [1088], replicated, may hold values from 0.1 to 1.9
- gain_two: float32 [1088], replicated, may hold values from 0.1 to 1.9
- qkv_down: bfloat16 [128, 1088], replicated, may hold values from -0.1875 to 0.1875
- qkv_up: bfloat16 [128, 3264], replicated, may hold values from -0.75 to 0.75
- out_down: bfloat16 [128, 1088], replicated, may hold values from -0.1875 to 0.1875
- out_up: bfloat16 [128, 1088], replicated, may hold values from -0.75 to 0.75
- fc1_down: bfloat16 [128, 1088], replicated, may hold values from -0.1875 to 0.1875
- fc1_up: bfloat16 [128, 4352], replicated, may hold values from -0.75 to 0.75
- fc2_down: bfloat16 [128, 4352], replicated, may hold values from -0.09375 to 0.09375
- fc2_up: bfloat16 [128, 1088], replicated, may hold values from -0.75 to 0.75
- cotangent: bfloat16 [16, 2048, 1088], P('dp', 'ctx'), may hold values from -6 to 6
Outputs:
- output: bfloat16 [16, 2048, 1088], P('dp', 'ctx')
- input_grad: bfloat16 [16, 2048, 1088], P('dp', 'ctx')
- qkv_down_grad: float32 [128, 1088], P('dp', 'ctx')
- qkv_up_grad: float32 [128, 3264], P('dp', 'ctx')
- out_down_grad: float32 [128, 1088], P('dp', 'ctx')
- out_up_grad: float32 [128, 1088], P('dp', 'ctx')
- fc1_down_grad: float32 [128, 1088], P('dp', 'ctx')
- fc1_up_grad: float32 [128, 4352], P('dp', 'ctx')
- fc2_down_grad: float32 [128, 4352], P('dp', 'ctx')
- fc2_up_grad: float32 [128, 1088], P('dp', 'ctx')
The draws below stay inside these ranges and needn't reach their ends.
Inputs may be any that keep to these rules, and one draw needn't show every extreme that they name: `segments`: document numbers never fall along a sequence; a document holds at most 1024 tokens.
All inputs are finite; a program needn't handle non-finite values.
Results may differ from the reference program's by a relative error of at most 0.023.
Values may be sent and summed in bfloat16 or wider, within the bound.
No kernel may reach another device: no remote copies, remote signals or barrier semaphores. Data moves between devices by JAX's collectives and lax.ppermute only.
A program may use at most 320 MiB of HBM per device.

```python
import math
import jax
import jax.numpy as jnp
import numpy as np
from jax import lax

D = 1088
HEADS = 17
FF = 4352
RANK = 16
ADAPTERS = 8
LEN = 2048
SEQS = 16


def place_ends(values, rng, low, largest):
    longest = values.shape.index(max(values.shape))
    spots = []
    for shift in (0, 1):
        where = [jax.random.randint(jax.random.fold_in(rng, axis), (), 0, length) for axis, length in enumerate(values.shape)]
        where[longest] = (where[longest] + shift) % values.shape[longest]
        spots.append(tuple(where))
    return values.at[spots[0]].set(low).at[spots[1]].set(largest)


def level_of(own_key, shape, split, smallest, top_value):
    factor_of, own = 1.0, jax.random.fold_in(own_key, 6)
    for dim, parts in split:
        heights = jnp.exp(jax.random.uniform(jax.random.fold_in(own, dim), (parts,), jnp.float32, smallest / len(split), top_value / len(split)))
        factor_of = factor_of * jnp.repeat(heights, shape[dim] // parts).reshape([-1 if axis == dim else 1 for axis in range(len(shape))])
    return factor_of


def split_up(count, total, reach, lean):
    loads = [(1 << 20) // math.isqrt(grade ** lean) + 1 for grade in range(2, count + 1)]
    surplus, given = total - reach - (count - 1), [1] * (count - 1)
    while surplus > 0:
        free = [i for i in range(count - 1) if given[i] < reach]
        whole, left = sum([loads[i] for i in free]), surplus
        for i in free:
            extra = min(reach - given[i], max(1, left * loads[i] // whole), surplus)
            given[i] = given[i] + extra
            surplus = surplus - extra
    return np.array([reach] + given)


def ragged(stream_key, amount, total, bound, skew):
    if amount == 2:
        one = jax.random.randint(stream_key, (), max(1, total - bound), min(bound, total - 1) + 1)
        return jnp.stack([one, total - one])
    lengths = jnp.asarray(split_up(amount, total, bound, skew), jnp.int32)
    pairs = (amount - 1) // 2
    source_of, receiver = lengths[1:1 + 2 * pairs:2], lengths[2:2 + 2 * pairs:2]
    slack = jnp.minimum(source_of - 1, bound - receiver)
    moved = jax.random.randint(jax.random.fold_in(stream_key, 1), (pairs,), 0, 1 << 20) % (slack + 1)
    lengths = lengths.at[1:1 + 2 * pairs:2].set(source_of - moved).at[2:2 + 2 * pairs:2].set(receiver + moved)
    return lengths[jax.random.permutation(jax.random.fold_in(stream_key, 2), amount)]


def scatter_about(own_key, extent, width, bound, cuts=(), kind=jnp.bfloat16):
    level = level_of(own_key, extent, cuts, -0.22, 0.18) if cuts else 1.0
    values = jax.random.normal(own_key, extent, jnp.float32) * width * level
    return jnp.minimum(jnp.maximum(values, -bound), bound).astype(kind)


def setup_inputs(seed: int = 0) -> dict:
    streams_of = jax.random.split(jax.random.key(seed), 19)
    return {
        "tokens": scatter_about(streams_of[0], (SEQS, LEN, D), 1.0, 6.0, ((0, 8), (1, 4))),
        "segments": jax.vmap(lambda own: jnp.searchsorted(jnp.cumsum(ragged(own, max(4, LEN // 64), LEN, LEN // 2, 2)), jnp.arange(LEN), side="right"))(jax.random.split(streams_of[1], SEQS)).reshape((SEQS, LEN)).astype(jnp.int32),
        "adapter_index": place_ends(jax.random.randint(streams_of[2], (SEQS,), 0, ADAPTERS), jax.random.fold_in(streams_of[2], 1), 0, ADAPTERS - 1).astype(jnp.int32),
        "w_qkv": scatter_about(streams_of[3], (D, 3 * D), D ** -0.5, 0.1875, ((0, 4), (1, 8))),
        "w_out": scatter_about(streams_of[4], (D, D), (D // 16) ** -0.5, 0.75, ((0, 4), (1, 8))),
        "w_fc1": scatter_about(streams_of[5], (D, FF), D ** -0.5, 0.1875, ((0, 4), (1, 8))),
        "w_fc2": scatter_about(streams_of[6], (FF, D), FF ** -0.5, 0.09375, ((0, 4), (1, 8))),
        "gain_one": jnp.clip(1.0 + 0.18 * jax.random.normal(streams_of[7], (D,), jnp.float32), 0.1, 1.9),
        "gain_two": jnp.clip(1.0 + 0.18 * jax.random.normal(streams_of[8], (D,), jnp.float32), 0.1, 1.9),
        "qkv_down": scatter_about(streams_of[9], (ADAPTERS * RANK, D), D ** -0.5, 0.1875),
        "qkv_up": scatter_about(streams_of[10], (ADAPTERS * RANK, 3 * D), (4 * RANK) ** -0.5, 0.75),
        "out_down": scatter_about(streams_of[11], (ADAPTERS * RANK, D), D ** -0.5, 0.1875),
        "out_up": scatter_about(streams_of[12], (ADAPTERS * RANK, D), (4 * RANK) ** -0.5, 0.75),
        "fc1_down": scatter_about(streams_of[13], (ADAPTERS * RANK, D), D ** -0.5, 0.1875),
        "fc1_up": scatter_about(streams_of[14], (ADAPTERS * RANK, FF), (4 * RANK) ** -0.5, 0.75),
        "fc2_down": scatter_about(streams_of[15], (ADAPTERS * RANK, FF), FF ** -0.5, 0.09375),
        "fc2_up": scatter_about(streams_of[16], (ADAPTERS * RANK, D), (4 * RANK) ** -0.5, 0.75),
        "cotangent": scatter_about(streams_of[17], (SEQS, LEN, D), 1.0, 6.0, ((0, 8), (1, 4))),
    }


eps = 1e-05
neg_big = -1e+30
highest = lax.Precision.HIGHEST

@jax.custom_vjp
def low(v):
    return lax.optimization_barrier(v.astype(jnp.bfloat16)).astype(jnp.float32)

@jax.custom_vjp
def low_back(v):
    return v

def low_keep(v):
    return (low(v), None)

def low_pass(kept, grad):
    return (grad,)

def back_keep(v):
    return (v, None)

def back_low(kept, grad):
    return (low(grad),)
low.defvjp(low_keep, low_pass)
low_back.defvjp(back_keep, back_low)

def matmul(left, right):
    return jnp.dot(left, right, precision=highest)

def normed(vector, gain):
    center = vector - lax.optimization_barrier(jnp.mean(vector, -1, keepdims=True))
    return center * lax.rsqrt(lax.optimization_barrier(jnp.mean(center * center, -1, keepdims=True)) + eps) * gain

def adapted(inputs, weight, down_rows, up_rows):
    lowered = low(low_back(matmul(inputs, down_rows.T)))
    return matmul(inputs, weight) + matmul(lowered, up_rows)

def attention(queries, keys, values, seg_ids):
    q_block = min(512, LEN)
    blocks = LEN // q_block
    head_dim = D // HEADS
    scale = head_dim ** (-0.5)
    key_pos = jnp.arange(LEN, dtype=jnp.int32)

    def one_block(block_items):
        query_part, query_seg, query_pos = block_items
        scores = low_back(jnp.einsum('qhd,khd->hqk', query_part, keys, precision=highest) * scale)
        allowed = (key_pos[None, :] <= query_pos[:, None]) & (seg_ids[None, :] == query_seg[:, None])
        scores = jnp.where(allowed[None], scores, neg_big)
        peak_score = lax.optimization_barrier(jnp.max(scores, -1, keepdims=True))
        expo_term = jnp.where(allowed[None], jnp.exp(scores - peak_score), 0.0)
        probs = expo_term / lax.optimization_barrier(jnp.sum(expo_term, -1, keepdims=True))
        return jnp.einsum('hqk,khd->qhd', low(probs), values, precision=highest)
    block_out = lax.map(jax.checkpoint(one_block), (queries.reshape(blocks, q_block, HEADS, head_dim), seg_ids.reshape(blocks, q_block), key_pos.reshape(blocks, q_block)))
    return block_out.reshape(LEN, D)

def layer(stream, seg_ids, weights, gains, adapts):
    w_qkv, w_out, w_fc1, w_fc2 = weights
    head_dim = D // HEADS
    normed_one = low(normed(stream, gains[0]))
    merged = low(low_back(adapted(normed_one, w_qkv, adapts[0], adapts[1])))
    queries = merged[:, :D].reshape(LEN, HEADS, head_dim)
    keys = merged[:, D:2 * D].reshape(LEN, HEADS, head_dim)
    values = merged[:, 2 * D:].reshape(LEN, HEADS, head_dim)
    mixed = low(low_back(attention(queries, keys, values, seg_ids)))
    branch = low_back(adapted(mixed, w_out, adapts[2], adapts[3]))
    middle = stream + branch
    normed_two = low(normed(middle, gains[1]))
    hidden = low_back(adapted(normed_two, w_fc1, adapts[4], adapts[5]))
    active = low(jax.nn.gelu(hidden, approximate=True))
    return middle + low_back(adapted(active, w_fc2, adapts[6], adapts[7]))

def reference(tokens, segments, adapter_index, w_qkv, w_out, w_fc1, w_fc2, gain_one, gain_two, qkv_down, qkv_up, out_down, out_up, fc1_down, fc1_up, fc2_down, fc2_up, cotangent):
    weights = tuple((matrix.astype(jnp.float32) for matrix in (w_qkv, w_out, w_fc1, w_fc2)))
    gains = (gain_one, gain_two)
    stacks = tuple((matrix.astype(jnp.float32).reshape(ADAPTERS, RANK, matrix.shape[1]) for matrix in (qkv_down, qkv_up, out_down, out_up, fc1_down, fc1_up, fc2_down, fc2_up)))

    def one_sequence(totals, seq_items):
        stream, seg_ids, adapter_id, grad_out = seq_items

        def forward(stack_list, stream_in):
            adapts = tuple((lax.dynamic_index_in_dim(stack, adapter_id, 0, keepdims=False) for stack in stack_list))
            return layer(stream_in, seg_ids, weights, gains, adapts)
        result, pull_back = jax.vjp(forward, stacks, stream.astype(jnp.float32))
        stack_grads, stream_grad = pull_back(grad_out.astype(jnp.float32))
        totals = tuple((total + grad for total, grad in zip(totals, stack_grads)))
        return (totals, (result.astype(jnp.bfloat16), stream_grad.astype(jnp.bfloat16)))
    start_totals = tuple((jnp.zeros(stack.shape, jnp.float32) for stack in stacks))
    totals, (outputs, input_grads) = lax.scan(one_sequence, start_totals, (tokens, segments, adapter_index.astype(jnp.int32), cotangent))
    flat = [total.reshape(ADAPTERS * RANK, total.shape[2]) for total in totals]
    return (outputs, input_grads, flat[0], flat[1], flat[2], flat[3], flat[4], flat[5], flat[6], flat[7])
```

```python
import functools

import jax
import jax.numpy as jnp
from jax import lax
from jax.experimental import pallas as pl
from jax.experimental.pallas import tpu as pltpu
from jax.sharding import PartitionSpec as P

HEADS = 17
ADAPTERS = 8
eps = 1e-05
neg_big = -1e30
BF = jnp.bfloat16
F32 = jnp.float32
BLK = 256
VMEM_LIMIT = 66000000


def nt(a, b):
    return lax.dot_general(a, b, (((1,), (1,)), ((), ())), preferred_element_type=F32)


def nn(a, b):
    return lax.dot_general(a, b, (((1,), (0,)), ((), ())), preferred_element_type=F32)


def tn(a, b):
    return lax.dot_general(a, b, (((0,), (0,)), ((), ())), preferred_element_type=F32)


def norm_rows(vector, gain):
    center = vector - jnp.mean(vector, -1, keepdims=True)
    inv_std = lax.rsqrt(jnp.mean(center * center, -1, keepdims=True) + eps)
    scaled = center * inv_std
    return (scaled * gain, scaled, inv_std)


def norm_back(grad, scaled, inv_std, gain):
    inner = grad * gain
    return inv_std * (
        inner
        - jnp.mean(inner, -1, keepdims=True)
        - scaled * jnp.mean(inner * scaled, -1, keepdims=True)
    )


def mask_bias(start_row, key_base, query_base, size):
    key_pos = lax.broadcasted_iota(jnp.int32, (size, size), 0) + key_base
    query_pos = lax.broadcasted_iota(jnp.int32, (size, size), 1) + query_base
    allowed = (key_pos >= start_row) & (key_pos <= query_pos)
    return jnp.where(allowed, 0.0, neg_big)


def attention_forward_kernel(
    parts, heads, head_dim, blk, first_ref, part_ref, start_ref, *refs
):
    pieces = refs[:parts]
    mixed_ref, flipped_ref, lse_ref = refs[parts : parts + 3]
    turned, keys, peak, total, accum = refs[parts + 3 :]
    wide = heads * head_dim
    local = pieces[0].shape[0]
    scale = head_dim ** (-0.5)
    for i in range(parts):
        base = part_ref[i] * local

        def load(c, _, i=i, base=base):
            rows = pl.ds(pl.multiple_of(c * blk, blk), blk)
            spot = pl.ds(pl.multiple_of(base + c * blk, blk), blk)
            block = pieces[i][rows, :]
            flip = block.T
            turned[:wide, spot] = flip[:wide] * scale
            turned[wide:, spot] = flip[2 * wide :]
            for h in range(heads):
                keys[h, spot, :] = block[:, wide + h * head_dim : wide + (h + 1) * head_dim]
            return 0

        lax.fori_loop(0, local // blk, load, 0)

    def query_block(i, _):
        cols = pl.ds(pl.multiple_of(i * blk, blk), blk)
        start_row = start_ref[:, cols]

        def visit(j, fresh):
            rows = pl.ds(pl.multiple_of(j * blk, blk), blk)
            bias = mask_bias(start_row, j * blk, i * blk, blk)
            for h in range(heads):
                band = slice(h * head_dim, (h + 1) * head_dim)
                below = slice(wide + h * head_dim, wide + (h + 1) * head_dim)
                scores = nn(keys[h, rows, :], turned[band, cols]) + bias
                top = jnp.max(scores, 0, keepdims=True)
                if fresh:
                    expo = jnp.exp(scores - top)
                    peak[h] = top
                    total[h] = jnp.sum(expo, 0, keepdims=True)
                    accum[band, :] = nn(turned[below, rows], expo.astype(BF))
                else:
                    old = peak[h]
                    new = jnp.maximum(old, top)
                    fade = jnp.exp(old - new)
                    expo = jnp.exp(scores - new)
                    peak[h] = new
                    total[h] = total[h] * fade + jnp.sum(expo, 0, keepdims=True)
                    accum[band, :] = accum[band, :] * fade + nn(
                        turned[below, rows], expo.astype(BF)
                    )

        visit(i, True)

        def more(k, _):
            visit(i - 1 - k, False)
            return 0

        lax.fori_loop(0, i - first_ref[i], more, 0)
        for h in range(heads):
            band = slice(h * head_dim, (h + 1) * head_dim)
            sums = total[h]
            lse_ref[h, :, cols] = peak[h] + jnp.log(sums)
            accum[band, :] = accum[band, :] * (1.0 / sums)
        low = accum[...].astype(BF)
        flipped_ref[:, cols] = low
        mixed_ref[cols, :] = low.T
        return 0

    lax.fori_loop(0, mixed_ref.shape[0] // blk, query_block, 0)


def attention_backward_kernel(
    parts, heads, head_dim, blk, first_ref, part_ref, start_ref, lse_ref, flipped_ref, *refs
):
    pieces = refs[:parts]
    grads = refs[parts : 2 * parts]
    out_ref = refs[2 * parts]
    turned, keys, values, grad_turned, delta, dq, dk, dv = refs[2 * parts + 1 :]
    wide = heads * head_dim
    local = pieces[0].shape[0]
    scale = head_dim ** (-0.5)
    for i in range(parts):
        base = part_ref[i] * local

        def load(c, _, i=i, base=base):
            rows = pl.ds(pl.multiple_of(c * blk, blk), blk)
            spot = pl.ds(pl.multiple_of(base + c * blk, blk), blk)
            block = pieces[i][rows, :]
            flip = block[:, : 2 * wide].T
            turned[:wide, spot] = flip[:wide] * scale
            turned[wide:, spot] = flip[wide:]
            gflip = grads[i][rows, :].T
            grad_turned[:, spot] = gflip
            product = gflip.astype(F32) * flipped_ref[:, spot].astype(F32)
            for h in range(heads):
                band = slice(h * head_dim, (h + 1) * head_dim)
                keys[h, spot, :] = block[:, wide + h * head_dim : wide + (h + 1) * head_dim]
                values[h, spot, :] = block[
                    :, 2 * wide + h * head_dim : 2 * wide + (h + 1) * head_dim
                ]
                delta[h, :, spot] = jnp.sum(product[band], 0, keepdims=True)
            return 0

        lax.fori_loop(0, local // blk, load, 0)
    dk[...] = jnp.zeros_like(dk)
    dv[...] = jnp.zeros_like(dv)

    def query_block(i, _):
        cols = pl.ds(pl.multiple_of(i * blk, blk), blk)
        start_row = start_ref[:, cols]
        dq[:, cols] = jnp.zeros((wide, blk), F32)

        def visit(k, _):
            j = i - k
            rows = pl.ds(pl.multiple_of(j * blk, blk), blk)
            bias = mask_bias(start_row, j * blk, i * blk, blk)
            for h in range(heads):
                band = slice(h * head_dim, (h + 1) * head_dim)
                below = slice(wide + h * head_dim, wide + (h + 1) * head_dim)
                queries = turned[band, cols]
                out_grad = grad_turned[band, cols]
                scores = nn(keys[h, rows, :], queries) + bias
                probs = jnp.exp(scores - lse_ref[h, :, cols])
                grad_probs = nn(values[h, rows, :], out_grad)
                grad_scores = (probs * (grad_probs - delta[h, :, cols])).astype(BF)
                dq[band, cols] += nn(turned[below, rows], grad_scores)
                dk[band, rows] += nt(queries, grad_scores)
                dv[band, rows] += nt(out_grad, probs.astype(BF))
            return 0

        lax.fori_loop(0, i - first_ref[i] + 1, visit, 0)
        return 0

    lax.fori_loop(0, start_ref.shape[1] // blk, query_block, 0)

    def finish(c, _):
        spot = pl.ds(pl.multiple_of(c * blk, blk), blk)
        out_ref[spot, :] = jnp.concatenate(
            [
                (dq[:, spot] * scale).astype(BF),
                dk[:, spot].astype(BF),
                dv[:, spot].astype(BF),
            ],
            0,
        ).T
        return 0

    lax.fori_loop(0, start_ref.shape[1] // blk, finish, 0)


def attention_forward(first, part_ids, start_row, pieces, heads, head_dim):
    parts, length = len(pieces), start_row.shape[1]
    wide = heads * head_dim
    blk = min(BLK, pieces[0].shape[0])
    smem, vmem = pl.BlockSpec(memory_space=pltpu.SMEM), pl.BlockSpec(memory_space=pltpu.VMEM)
    area = heads * length * 640
    return pl.pallas_call(
        functools.partial(attention_forward_kernel, parts, heads, head_dim, blk),
        out_shape=(
            jax.ShapeDtypeStruct((length, wide), BF),
            jax.ShapeDtypeStruct((wide, length), BF),
            jax.ShapeDtypeStruct((heads, 1, length), F32),
        ),
        in_specs=[smem, smem] + [vmem] * (1 + parts),
        out_specs=(vmem, vmem, vmem),
        scratch_shapes=[
            pltpu.VMEM((2 * wide, length), BF),
            pltpu.VMEM((heads, length, head_dim), BF),
            pltpu.VMEM((heads, 1, blk), F32),
            pltpu.VMEM((heads, 1, blk), F32),
            pltpu.VMEM((wide, blk), F32),
        ],
        compiler_params=pltpu.CompilerParams(vmem_limit_bytes=VMEM_LIMIT),
        cost_estimate=pl.CostEstimate(
            flops=area * 1024, bytes_accessed=10 * length * wide, transcendentals=area
        ),
        name="attention_forward",
    )(first, part_ids, start_row, *pieces)


def attention_backward(first, part_ids, start_row, lse, flipped, pieces, grads, heads, head_dim):
    parts, length = len(pieces), start_row.shape[1]
    wide = heads * head_dim
    blk = min(BLK, pieces[0].shape[0])
    smem, vmem = pl.BlockSpec(memory_space=pltpu.SMEM), pl.BlockSpec(memory_space=pltpu.VMEM)
    area = heads * length * 640
    return pl.pallas_call(
        functools.partial(attention_backward_kernel, parts, heads, head_dim, blk),
        out_shape=jax.ShapeDtypeStruct((length, 3 * wide), BF),
        in_specs=[smem, smem] + [vmem] * (3 + 2 * parts),
        out_specs=vmem,
        scratch_shapes=[
            pltpu.VMEM((2 * wide, length), BF),
            pltpu.VMEM((heads, length, head_dim), BF),
            pltpu.VMEM((heads, length, head_dim), BF),
            pltpu.VMEM((wide, length), BF),
            pltpu.VMEM((heads, 1, length), F32),
            pltpu.VMEM((wide, length), F32),
            pltpu.VMEM((wide, length), F32),
            pltpu.VMEM((wide, length), F32),
        ],
        compiler_params=pltpu.CompilerParams(vmem_limit_bytes=VMEM_LIMIT),
        cost_estimate=pl.CostEstimate(
            flops=area * 2560, bytes_accessed=16 * length * wide, transcendentals=area
        ),
        name="attention_backward",
    )(first, part_ids, start_row, lse, flipped, *pieces, *grads)


def per_device(
    dp_size,
    ctx_size,
    tokens,
    segments,
    adapter_index,
    w_qkv,
    w_out,
    w_fc1,
    w_fc2,
    gain_one,
    gain_two,
    qkv_down,
    qkv_up,
    out_down,
    out_up,
    fc1_down,
    fc1_up,
    fc2_down,
    fc2_up,
    cotangent,
):
    both = ("dp", "ctx")
    seqs, rows, width = tokens.shape
    length = segments.shape[1]
    head_dim = width // HEADS
    rank = qkv_down.shape[0] // ADAPTERS
    group = ctx_size // seqs
    local = seqs * rows
    heads = -(-HEADS // group)
    wide = heads * head_dim
    ratio = w_fc2.shape[0] // w_fc1.shape[0]
    cut = w_fc1.shape[0]
    hidden_size = fc1_up.shape[1]

    dp_at, ctx_at = lax.axis_index("dp"), lax.axis_index("ctx")
    core_at = dp_at % 2
    place = ctx_at * 2 + core_at
    seq_at, part_at = place // group, place % group

    def send(value, route):
        pairs = []
        for d in range(dp_size):
            for z in range(ctx_size):
                d2, z2 = route(d, z)
                pairs.append((d * ctx_size + z, d2 * ctx_size + z2))
        return lax.ppermute(value, both, pairs)

    def to_sequence(p):
        def route(d, z):
            q = (d % 2) * seqs + (z + p) % seqs
            e = q * group + z // seqs
            return (d // 2) * 2 + e % 2, e // 2

        return route

    def from_sequence(p):
        def route(d, z):
            e = 2 * z + d % 2
            q, r = e // group, e % group
            t = (q - p) % seqs
            return (d // 2) * 2 + q // seqs, r * seqs + t

        return route

    def within_group(m):
        def route(d, z):
            e = 2 * z + d % 2
            e2 = (e // group) * group + (e % group ^ m)
            return (d // 2) * 2 + e2 % 2, e2 // 2

        return route

    def pick(stack, index):
        return lax.dynamic_index_in_dim(stack, index, 0, keepdims=False)

    def spread_tokens(block):
        got = [
            send(pick(block, (ctx_at + p) % seqs), to_sequence(p)) for p in range(seqs)
        ]
        stacked = jnp.stack(got)
        return jnp.concatenate(
            [pick(stacked, (seq_at - t) % seqs) for t in range(seqs)], 0
        )

    def return_tokens(block):
        shaped = block.reshape(seqs, rows, width)
        got = [
            send(pick(shaped, (seq_at - p) % seqs), from_sequence(p)) for p in range(seqs)
        ]
        stacked = jnp.stack(got)
        return jnp.stack([pick(stacked, (j - ctx_at) % seqs) for j in range(seqs)])

    def gather_rows(shard):
        got = [shard] + [
            send(shard, lambda d, z, k=k: (d, (z + k) % ctx_size))
            for k in range(1, ctx_size)
        ]
        cycle = jnp.stack(got[:0:-1] + got[:1] + got[:0:-1])
        ordered = lax.dynamic_slice_in_dim(cycle, ctx_size - 1 - ctx_at, ctx_size, 0)
        return ordered.reshape(ctx_size * shard.shape[0], shard.shape[1]).T

    plane_bits = []
    bit = 2
    while bit < dp_size:
        plane_bits.append(bit)
        bit *= 2
    half_bits = len(plane_bits) // 2

    def join(mine, other, bit):
        low = (dp_at // bit) % 2 == 0
        return jnp.stack([jnp.where(low, mine, other), jnp.where(low, other, mine)])

    def gather_columns(block):
        n = block.shape[0]
        first = -(-n // 16) * 8
        done = []
        for piece, order in (
            (block[:first], plane_bits),
            (block[first:], plane_bits[half_bits:] + plane_bits[:half_bits]),
        ):
            held, axes = piece[None], []
            for b in order:
                other = send(held, lambda d, z, b=b: (d ^ b, z))
                held = join(held, other, b)
                axes = [b] + axes
                held = held.reshape((2,) * len(axes) + piece.shape)
            wanted = sorted(axes, reverse=True)
            held = held.transpose([axes.index(b) for b in wanted] + [len(axes), len(axes) + 1])
            done.append(held.reshape((dp_size // 2,) + piece.shape))
        held = jnp.concatenate(done, 1)
        other = send(held, lambda d, z: (d ^ 1, z))
        low = core_at == 0
        return jnp.stack([jnp.where(low, held, other), jnp.where(low, other, held)], 1).reshape(
            dp_size, n, width
        )

    turned_qkv = gather_columns(gather_rows(w_qkv)).reshape(-1, width)
    sequence_in = spread_tokens(tokens)
    cols_out, cols_fc1, cols_fc2 = w_out.shape[1], w_fc1.shape[1], w_fc2.shape[1]
    rest_shard = jnp.concatenate(
        [w_out, w_fc1]
        + [w_fc2[b * cut : (b + 1) * cut] for b in range(ratio)],
        1,
    )
    rest = gather_columns(gather_rows(rest_shard))
    turned_out = rest[:, :cols_out].reshape(-1, width)
    turned_fc1 = (
        rest[:, cols_out : cols_out + cols_fc1]
        .reshape(ctx_size, ratio, cut, width)
        .transpose(1, 0, 2, 3)
        .reshape(hidden_size, width)
    )
    at = cols_out + cols_fc1
    turned_fc2 = [
        rest[:, at + b * cols_fc2 : at + (b + 1) * cols_fc2].reshape(width, width)
        for b in range(ratio)
    ]

    table = jnp.concatenate([segments, adapter_index[:, None]], 1)
    other_table = send(table, lambda d, z: (d ^ 1, z))
    low = core_at == 0
    tables = jnp.concatenate(
        [jnp.where(low, table, other_table), jnp.where(low, other_table, table)], 0
    )
    own_table = pick(tables, seq_at)
    seg, adapter = own_table[:length], own_table[length]
    column_adapters = tables[:, length]
    start_row = jnp.sum(
        (seg[:, None] < seg[None, :]).astype(jnp.int32), 0, dtype=jnp.int32
    )[None]
    blk = min(BLK, local)
    first = start_row[0, ::blk] // blk
    part_ids = jnp.stack([part_at ^ m for m in range(group)]).astype(jnp.int32)

    def chosen(stack):
        return lax.dynamic_slice_in_dim(stack, adapter * rank, rank, 0)

    d_qkv, u_qkv, d_out, u_out, d_fc1, u_fc1, d_fc2, u_fc2 = [
        chosen(s)
        for s in (qkv_down, qkv_up, out_down, out_up, fc1_down, fc1_up, fc2_down, fc2_up)
    ]

    def by_group(matrix):
        tail = matrix.shape[1]
        shaped = matrix.reshape(3, HEADS, head_dim, tail)
        shaped = jnp.pad(shaped, ((0, 0), (0, group * heads - HEADS), (0, 0), (0, 0)))
        return (
            shaped.reshape(3, group, wide, tail)
            .transpose(1, 0, 2, 3)
            .reshape(group, 3 * wide, tail)
        )

    grouped_qkv = by_group(turned_qkv)
    grouped_up = by_group(u_qkv.T)

    def by_block(matrix):
        return (
            matrix.reshape(rank, ctx_size, ratio, cut)
            .transpose(0, 2, 1, 3)
            .reshape(rank, hidden_size)
        )

    u_fc1, d_fc2 = by_block(u_fc1), by_block(d_fc2)

    stream = sequence_in.astype(F32)
    normed_one, scaled_one, inv_one = norm_rows(stream, gain_one)
    normed_one = normed_one.astype(BF)
    low_qkv = nt(normed_one, d_qkv).astype(BF)
    merged = jnp.stack(
        [
            (nt(normed_one, grouped_qkv[g]) + nt(low_qkv, grouped_up[g])).astype(BF)
            for g in range(group)
        ]
    )
    pieces = [pick(merged, part_at)] + [
        send(pick(merged, part_at ^ m), within_group(m)) for m in range(1, group)
    ]
    mixed, flipped, lse = attention_forward(first, part_ids, start_row, pieces, heads, head_dim)
    mixed = mixed.reshape(group, local, wide)

    def collect(parts_of):
        got = [pick(parts_of, part_at)] + [
            send(pick(parts_of, part_at ^ m), within_group(m)) for m in range(1, group)
        ]
        stacked = jnp.stack(got)
        return [pick(stacked, part_at ^ g) for g in range(group)]

    attended = jnp.concatenate(collect(mixed), 1)[:, :width]
    low_out = nt(attended, d_out).astype(BF)
    middle = stream + nt(attended, turned_out) + nn(low_out, u_out)
    normed_two, scaled_two, inv_two = norm_rows(middle, gain_two)
    normed_two = normed_two.astype(BF)
    low_fc1 = nt(normed_two, d_fc1).astype(BF)
    hidden = nt(normed_two, turned_fc1) + nn(low_fc1, u_fc1)
    active = jax.nn.gelu(hidden, approximate=True).astype(BF)
    low_fc2 = nt(active, d_fc2).astype(BF)
    mlp = nn(low_fc2, u_fc2)
    for b in range(ratio):
        mlp = mlp + nt(active[:, b * width : (b + 1) * width], turned_fc2[b])
    output = return_tokens((middle + mlp).astype(BF))

    grad_out = spread_tokens(cotangent)
    grad_low_fc2 = nt(grad_out, u_fc2).astype(BF)
    grad_active = jnp.concatenate(
        [nn(grad_out, turned_fc2[b]) for b in range(ratio)], 1
    ) + nn(grad_low_fc2, d_fc2)
    grad_fc2_up = tn(low_fc2, grad_out)
    grad_fc2_down = tn(grad_low_fc2, active)
    _, gelu_pull = jax.vjp(lambda v: jax.nn.gelu(v, approximate=True), hidden)
    grad_hidden = gelu_pull(grad_active)[0].astype(BF)
    grad_low_fc1 = nt(grad_hidden, u_fc1).astype(BF)
    grad_two = nn(grad_hidden, turned_fc1) + nn(grad_low_fc1, d_fc1)
    grad_fc1_up = tn(low_fc1, grad_hidden)
    grad_fc1_down = tn(grad_low_fc1, normed_two)
    grad_middle = grad_out.astype(F32) + norm_back(grad_two, scaled_two, inv_two, gain_two)
    grad_branch = grad_middle.astype(BF)
    grad_low_out = nt(grad_branch, u_out).astype(BF)
    grad_att = (nn(grad_branch, turned_out) + nn(grad_low_out, d_out)).astype(BF)
    grad_out_up = tn(low_out, grad_branch)
    grad_out_down = tn(grad_low_out, attended)

    padded = jnp.pad(grad_att, ((0, 0), (0, group * wide - width)))
    by_heads = padded.reshape(local, group, wide).transpose(1, 0, 2)
    grad_pieces = [pick(by_heads, part_at)] + [
        send(pick(by_heads, part_at ^ m), within_group(m)) for m in range(1, group)
    ]
    grad_parts = attention_backward(
        first, part_ids, start_row, lse, flipped, pieces, grad_pieces, heads, head_dim
    ).reshape(group, local, 3 * wide)
    grad_groups = collect(grad_parts)
    grad_low_qkv = sum(nn(grad_groups[g], grouped_up[g]) for g in range(group)).astype(BF)
    grad_one = nn(grad_low_qkv, d_qkv)
    for g in range(group):
        grad_one = grad_one + nn(grad_groups[g], grouped_qkv[g])
    grad_qkv_down = tn(grad_low_qkv, normed_one)
    up_groups = jnp.stack([tn(low_qkv, grad_groups[g]) for g in range(group)], 1)
    grad_qkv_up = (
        up_groups.reshape(rank, group, 3, wide)
        .transpose(0, 2, 1, 3)
        .reshape(rank, 3, group * wide)[:, :, :width]
        .reshape(rank, 3 * width)
    )
    input_grad = return_tokens(
        (grad_middle + norm_back(grad_one, scaled_one, inv_one, gain_one)).astype(BF)
    )

    def plain(grad):
        return grad.reshape(rank, ctx_size, grad.shape[1] // ctx_size).transpose(1, 0, 2)

    def blocked(grad):
        return (
            grad.reshape(rank, ratio, ctx_size, cut)
            .transpose(2, 0, 1, 3)
            .reshape(ctx_size, rank, ratio * cut)
        )

    owners = jnp.stack(
        [
            pick(column_adapters, (((ctx_at - k) % ctx_size) * 2 + core_at) // group)
            for k in range(ctx_size)
        ]
    )
    onehot = (owners[:, None] == jnp.arange(ADAPTERS, dtype=jnp.int32)[None]).astype(F32)

    def reduce_terms(terms):
        packed = jnp.concatenate(terms, 2).astype(BF)
        got = [pick(packed, ctx_at)] + [
            send(
                pick(packed, (ctx_at + k) % ctx_size),
                lambda d, z, k=k: (d, (z + k) % ctx_size),
            )
            for k in range(1, ctx_size)
        ]
        laid = sum(
            onehot[k][:, None, None] * got[k].astype(F32)[None] for k in range(ctx_size)
        ).reshape(dp_size, ADAPTERS * rank // dp_size, packed.shape[2])
        mine = pick(laid, dp_at)
        low_laid = laid.astype(BF)
        for m in range(1, dp_size):
            mine = mine + send(
                pick(low_laid, dp_at ^ m), lambda d, z, m=m: (d ^ m, z)
            ).astype(F32)
        sizes = [t.shape[2] for t in terms]
        ends = [sum(sizes[: i + 1]) for i in range(len(sizes))]
        return [mine[:, e - s : e] for e, s in zip(ends, sizes)]

    od, ou, f1d, f1u, f2d, f2u = reduce_terms(
        [
            plain(grad_out_down),
            plain(grad_out_up),
            plain(grad_fc1_down),
            blocked(grad_fc1_up),
            blocked(grad_fc2_down),
            plain(grad_fc2_up),
        ]
    )
    qd, qu = reduce_terms([plain(grad_qkv_down), plain(grad_qkv_up)])
    return (output, input_grad, qd, qu, od, ou, f1d, f1u, f2d, f2u)


def solution(mesh):
    shape = dict(mesh.shape)
    return jax.shard_map(
        functools.partial(per_device, shape["dp"], shape["ctx"]),
        mesh=mesh,
        in_specs=(
            P("dp", "ctx", None),
            P("dp", None),
            P("dp"),
            P("ctx", "dp"),
            P("ctx", "dp"),
            P("ctx", "dp"),
            P("ctx", "dp"),
        )
        + (P(),) * 10
        + (P("dp", "ctx", None),),
        out_specs=(P("dp", "ctx", None), P("dp", "ctx", None)) + (P("dp", "ctx"),) * 8,
        check_vma=False,
    )
```
